32 devices in a mesh: slides: 2 (over x), tok: 16 (over z, y, core).
Axes of the slice: x: 2, y: 2, z: 4, core: 2. Of those that a mesh axis runs over, the one named last changes fastest.
Arguments:
- queries: bfloat16 [8, 2048, 768], P('slides', 'tok'), parts along dimension 0, may hold values from -7 to 7
- key_rows: bfloat16 [8, 2048, 768], P('slides', 'tok'), parts along dimension 0, may hold values from -6 to 6
- value_rows: bfloat16 [8, 2048, 768], P('slides', 'tok'), parts along dimension 0, may hold values from -6 to 6
- projected_output_gradient: bfloat16 [8, 32768, 768], P('slides', 'tok'), parts along dimension 0, may hold values from -24 to 24
- out_weight: bfloat16 [768, 768], replicated, may hold values from -0.21875 to 0.21875
- offsets: int32 [16], replicated, may hold values from 0 to 15, each once
Outputs:
- grad_queries: bfloat16 [8, 2048, 768], P('slides', 'tok'), parts along dimension 0
- grad_keys: bfloat16 [8, 2048, 768], P('slides', 'tok'), parts along dimension 0
- grad_values: bfloat16 [8, 2048, 768], P('slides', 'tok'), parts along dimension 0
- grad_weight: float32 [1536, 768], P(('slides', 'tok')), parts along dimension 0
The draws below stay inside these ranges and needn't reach their ends.
There are 2 independent parts, one for each index of `slides`. The reference program is written for one: setup_inputs(seed, part) draws one part's arguments, and reference() takes and returns one part's arrays. A program takes and returns all parts, laid end to end along the dimension named above; an argument that names none is the same for every part. Nothing has to cross between parts.
Inputs may be any that keep to these rules, and one draw needn't show every extreme that they name: offsets names each of the 16 phases once.
All inputs are finite; a program needn't handle non-finite values.
Results may differ from the reference program's by a relative error of at most 0.014.
Values may be sent and summed in bfloat16 or wider, within the bound.
A program may use at most 192 MiB of HBM per device.

```python
import jax
import jax.numpy as jnp
from jax import lax

D = 768
HEADS = 16
DILATION_RATE = 16
ROUNDS = 4
ROWS = 2048
TOKENS = 32768
N_TOK = 16


def draw_queries(key, part):
    shape_all = (ROUNDS, ROWS, D)
    drawn = jnp.clip(jax.random.normal(jax.random.fold_in(key, 11), shape_all, jnp.float32), -5.0, 5.0)
    return drawn.astype(jnp.bfloat16)


def draw_key_rows(key, part):
    shape_all = (ROUNDS, ROWS, D)
    drawn = jnp.clip(jax.random.normal(jax.random.fold_in(key, 21), shape_all, jnp.float32), -5.0, 5.0)
    return drawn.astype(jnp.bfloat16)


def raised(values, stream_key, source, target, parts, factor):
    owner, partner = [(jnp.arange(values.shape[dim]) // (values.shape[dim] // parts)).reshape([-1 if axis == dim else 1 for axis in range(values.ndim)]) for dim in (source, target)]
    chosen = jax.random.permutation(stream_key, parts)[partner]
    strong = (owner == chosen) | (owner == (partner + parts // 2) % parts)
    return jnp.where(strong, factor * values, values)


def block_levels(own_key, shape, shards, least, top_value):
    factor_of, own = 1.0, jax.random.fold_in(own_key, 6)
    for dim, parts in shards:
        steps = jnp.exp(jax.random.uniform(jax.random.fold_in(own, dim), (parts,), jnp.float32, least / len(shards), top_value / len(shards)))
        factor_of = factor_of * jnp.repeat(steps, shape[dim] // parts).reshape([-1 if axis == dim else 1 for axis in range(len(shape))])
    return factor_of


def scatter_about(key, shape, scale, most, shards=(), kind=jnp.bfloat16):
    values = scale * jax.random.normal(key, shape, jnp.float32)
    if shards:
        values = values * block_levels(key, shape, shards, -0.22, 0.18)
    return jnp.clip(values, -most, most).astype(kind)


def heavy_noise(stream_key, shape, scale, bound, pieces, heavy, kind=jnp.bfloat16):
    values = scale * jax.random.normal(stream_key, shape, jnp.float32)
    if pieces:
        values = values * block_levels(stream_key, shape, pieces, -0.22, 0.18)
    return jnp.clip(raised(values, jax.random.fold_in(stream_key, 3), *heavy), -bound, bound).astype(kind)


def setup_inputs(seed: int = 0, part: int = 0) -> dict:
    key_of = jax.random.split(jax.random.key(seed), 7)
    part_keys = jax.random.split(jax.random.fold_in(key_of[6], part), 7)
    return {
        "queries": draw_queries(jax.random.fold_in(jax.random.fold_in(key_of[6], part), 71), part),
        "key_rows": draw_key_rows(jax.random.fold_in(jax.random.fold_in(key_of[6], part), 71), part),
        "value_rows": scatter_about(part_keys[2], (ROUNDS, ROWS, D), 1.0, 6.0, ((1, 16),)),
        "projected_output_gradient": heavy_noise(part_keys[3], (ROUNDS, TOKENS, D), 4.0, 24.0, ((1, 16),), (1, 2, 16, 2.0)),
        "out_weight": scatter_about(key_of[4], (D, D), D ** -0.5, 0.21875),
        "offsets": jax.random.permutation(key_of[5], DILATION_RATE).astype(jnp.int32),
    }


def attend(query_blk, key_blk, value_blk, grad_blk):
    score_scale = query_blk.shape[1] ** -0.5
    scores = jnp.dot(query_blk, key_blk.T, preferred_element_type=jnp.float32) * score_scale
    top_score = jnp.max(scores, axis=1, keepdims=True)
    expo = jnp.exp(scores - top_score)
    probs = expo / jnp.sum(expo, axis=1, keepdims=True)
    probs_low = probs.astype(jnp.bfloat16)
    attn_out = lax.optimization_barrier(jnp.dot(probs_low, value_blk, preferred_element_type=jnp.float32).astype(jnp.bfloat16))
    dprobs = jnp.dot(grad_blk, value_blk.T, preferred_element_type=jnp.float32)
    delta = jnp.sum(grad_blk.astype(jnp.float32) * attn_out.astype(jnp.float32), axis=1, keepdims=True)
    dscores = (probs * (dprobs - delta)).astype(jnp.bfloat16)
    grad_query = (jnp.dot(dscores, key_blk, preferred_element_type=jnp.float32) * score_scale).astype(jnp.bfloat16)
    grad_key = (jnp.dot(dscores.T, query_blk, preferred_element_type=jnp.float32) * score_scale).astype(jnp.bfloat16)
    grad_value = jnp.dot(probs_low.T, grad_blk, preferred_element_type=jnp.float32).astype(jnp.bfloat16)
    return grad_query, grad_key, grad_value, attn_out


def reference(queries, key_rows, value_rows, projected_output_gradient, out_weight, offsets):
    rounds, row_total_count, feature_width = queries.shape
    heads = HEADS
    head_dim = feature_width // heads
    segments = N_TOK // 16
    seg_rows = row_total_count // segments
    weight_split = out_weight.reshape(feature_width, heads, head_dim).astype(jnp.float32)

    def split_heads(array):
        return array.reshape(segments, seg_rows, heads, head_dim).transpose(0, 2, 1, 3).reshape(segments * heads, seg_rows, head_dim)

    def join_heads(array):
        return array.reshape(segments, heads, seg_rows, head_dim).transpose(0, 2, 1, 3).reshape(row_total_count, feature_width)

    grad_q_list = []
    grad_k_list = []
    grad_v_list = []
    weight_total = jnp.zeros((feature_width, feature_width), jnp.float32)
    for round_position in range(rounds):
        phase_shifted = projected_output_gradient[round_position].reshape(row_total_count, DILATION_RATE, feature_width)
        chosen = phase_shifted[:, offsets.astype(jnp.int32), :]
        grad_heads = jnp.einsum('ihj,jhe->ihe', chosen.astype(jnp.float32), weight_split)
        grad_heads = lax.optimization_barrier(grad_heads.astype(jnp.bfloat16)).reshape(row_total_count, feature_width)
        items = (split_heads(queries[round_position]), split_heads(key_rows[round_position]), split_heads(value_rows[round_position]), split_heads(grad_heads))
        grad_query, grad_key, grad_value, attn_out = lax.map(lambda item: attend(*item), items)
        grad_q_list.append(join_heads(grad_query))
        grad_k_list.append(join_heads(grad_key))
        grad_v_list.append(join_heads(grad_value))
        attn_rows = join_heads(attn_out).reshape(row_total_count, heads, head_dim)
        term = jnp.einsum('ihj,ihe->jhe', chosen.astype(jnp.float32), attn_rows.astype(jnp.float32))
        weight_total = weight_total + term.reshape(feature_width, feature_width)
    return jnp.stack(grad_q_list), jnp.stack(grad_k_list), jnp.stack(grad_v_list), weight_total
```

```python
import functools

import jax
import jax.numpy as jnp
from jax import lax
from jax.experimental import pallas as pl
from jax.experimental.pallas import tpu as pltpu
from jax.sharding import PartitionSpec as P

MESH = pl.DeviceIdType.MESH
F32 = jnp.float32
BF16 = jnp.bfloat16
LOG2E = 1.4426950408889634


def dot(a, b, ca, cb):
    return lax.dot_general(a, b, (((ca,), (cb,)), ((), ())), preferred_element_type=F32)


def flip_bits(index, mask):
    out = index
    bit = 1
    while bit <= mask:
        if mask & bit:
            out = out + bit - 2 * bit * ((index // bit) % 2)
        bit *= 2
    return out


def main_kernel(
    dims,
    q_ref, k_ref, v_ref, w_ref, mask_ref, x_hbm,
    dq_ref, dk_ref, dv_ref, gw_ref,
    x, out_t, recv, res, ret, g_rows, spread, k_rows, v_rows, dk_acc, dv_acc, term, half, part, landed,
    x_sem, qkv_send, qkv_recv, g_send, g_recv, res_send, ret_recv, red_send, red_recv,
):
    rounds, rows, width, heads, head_dim, tok, phases = dims
    seg = heads * rows
    me = lax.axis_index("tok")
    lane = me % heads
    base = me - lane
    order = sorted(range(1, heads), key=lambda s: (-(s // (heads // 2)), -s))
    scale = head_dim ** (-0.5)

    for r in range(rounds):
        pltpu.make_async_copy(x_hbm.at[r], x.at[r], x_sem.at[r]).start()

    greet = sorted(set(flip_bits_plain(heads)) | set(b for b in bits_of(tok)))
    barrier = pltpu.get_barrier_semaphore()
    for s in greet:
        peer = flip_bits(me, s)
        pl.semaphore_signal(barrier, inc=1, device_id={"tok": peer}, device_id_type=MESH)
    pl.semaphore_wait(barrier, len(greet))

    def columns(d):
        return pl.ds(pl.multiple_of(d * rows, rows), rows)

    def send_out(r, first, count, send_sem, recv_sem):
        for s in order:
            d = flip_bits(lane, s)
            pltpu.make_async_remote_copy(
                src_ref=out_t.at[r, pl.ds(first, count), d],
                dst_ref=recv.at[r, pl.ds(first, count), :, columns(lane)],
                send_sem=send_sem.at[r],
                recv_sem=recv_sem.at[r],
                device_id={"tok": base + d},
                device_id_type=MESH,
            ).start()
        pltpu.make_async_copy(
            out_t.at[r, pl.ds(first, count), lane],
            recv.at[r, pl.ds(first, count), :, columns(lane)],
            recv_sem.at[r],
        ).start()

    def prepare(r, carry):
        for a, ref in enumerate((q_ref, k_ref, v_ref)):
            out_t[r, a] = ref[r].T.reshape(heads, head_dim, rows)
        send_out(r, 0, 3, qkv_send, qkv_recv)
        pltpu.make_async_copy(x_hbm.at[r], x.at[r], x_sem.at[r]).wait()

        def chunk(c, inner):
            t = pl.multiple_of(c * 256, 256)
            y = dot(x[r, pl.ds(t, 256), :], w_ref[...], 1, 0)
            y = y.reshape(256 // phases, phases, width) * mask_ref[...][None]
            i = pl.multiple_of(c * (256 // phases), 256 // phases)
            g_rows[pl.ds(i, 256 // phases), :] = jnp.sum(y, axis=1).astype(BF16)
            return inner

        lax.fori_loop(0, rows * phases // 256, chunk, 0)
        out_t[r, 3] = g_rows[...].T.reshape(heads, head_dim, rows)
        send_out(r, 3, 1, g_send, g_recv)
        return carry

    lax.fori_loop(0, rounds, prepare, 0)

    block = 256

    def attend(r, carry):
        pltpu.make_async_copy(
            recv.at[r, pl.ds(0, 3)], recv.at[r, pl.ds(0, 3)], qkv_recv.at[r]
        ).wait()
        k_rows[...] = recv[r, 1].T
        v_rows[...] = recv[r, 2].T
        dk_acc[...] = jnp.zeros_like(dk_acc)
        dv_acc[...] = jnp.zeros_like(dv_acc)
        pltpu.make_async_copy(recv.at[r, 3], recv.at[r, 3], g_recv.at[r]).wait()

        def q_block(b, inner):
            cols = pl.ds(pl.multiple_of(b * block, block), block)
            qt = recv[r, 0, :, cols]
            gt = recv[r, 3, :, cols]
            s = dot(k_rows[...], qt, 1, 0)
            top = jnp.max(s, axis=0, keepdims=True)
            e = jnp.exp2((s - top) * (scale * LOG2E))
            inv = 1.0 / jnp.sum(e, axis=0, keepdims=True)
            p = e * inv
            p_low = p.astype(BF16)
            ot = dot(recv[r, 2], p_low, 1, 0).astype(BF16)
            res[r, 3, :, cols] = ot
            dp = dot(v_rows[...], gt, 1, 0)
            delta = jnp.sum(gt.astype(F32) * ot.astype(F32), axis=0, keepdims=True)
            ds = (p * (dp - delta)).astype(BF16)
            res[r, 0, :, cols] = (dot(recv[r, 1], ds, 1, 0) * scale).astype(BF16)
            dk_acc[...] += dot(qt, ds, 1, 1)
            dv_acc[...] += dot(gt, p_low, 1, 1)
            return inner

        lax.fori_loop(0, seg // block, q_block, 0)
        res[r, 1] = (dk_acc[...] * scale).astype(BF16)
        res[r, 2] = dv_acc[...].astype(BF16)
        for s in order:
            d = flip_bits(lane, s)
            pltpu.make_async_remote_copy(
                src_ref=res.at[r, :, :, columns(d)],
                dst_ref=ret.at[r, :, lane],
                send_sem=res_send.at[r],
                recv_sem=ret_recv.at[r],
                device_id={"tok": base + d},
                device_id_type=MESH,
            ).start()
        pltpu.make_async_copy(
            res.at[r, :, :, columns(lane)], ret.at[r, :, lane], ret_recv.at[r]
        ).start()
        return carry

    lax.fori_loop(0, rounds, attend, 0)

    term[...] = jnp.zeros_like(term)
    jb = 256

    def finish(r, carry):
        pltpu.make_async_copy(ret.at[r], ret.at[r], ret_recv.at[r]).wait()
        g_rows[...] = ret[r, 3].reshape(width, rows).T

        def chunk(c, inner):
            n = 256 // phases
            a = g_rows[pl.ds(pl.multiple_of(c * n, n), n), :].astype(F32)
            full = a[:, None, :] * mask_ref[...][None]
            spread[pl.ds(pl.multiple_of(c * 256, 256), 256), :] = full.reshape(256, width).astype(BF16)
            return inner

        lax.fori_loop(0, rows * phases // 256, chunk, 0)

        for j in range(width // jb):
            here = pl.ds(j * jb, jb)
            term[here, :] += dot(x[r, :, here], spread[...], 0, 0)
        for a, ref in enumerate((dq_ref, dk_ref, dv_ref)):
            ref[r] = ret[r, a].reshape(width, rows).T
        return carry

    lax.fori_loop(0, rounds, finish, 0)

    own = width // tok
    part[...] = term[...].reshape(tok, own, width)
    count = tok
    stage = 0
    bit = 1
    at = 0
    kept = 0
    while bit < tok:
        b = (me // bit) % 2
        peer = me + bit - 2 * bit * b
        count //= 2
        for u in range(count):
            half[at + u] = part[kept + bit * (1 - b) + 2 * bit * u].astype(BF16)
        for u in range(count):
            pltpu.make_async_remote_copy(
                src_ref=half.at[at + u],
                dst_ref=landed.at[at + u],
                send_sem=red_send.at[at + u],
                recv_sem=red_recv.at[at + u],
                device_id={"tok": peer},
                device_id_type=MESH,
            ).start()
        kept = kept + bit * b
        for u in range(count):
            pltpu.make_async_remote_copy(
                src_ref=half.at[at + u],
                dst_ref=landed.at[at + u],
                send_sem=red_send.at[at + u],
                recv_sem=red_recv.at[at + u],
                device_id={"tok": peer},
                device_id_type=MESH,
            ).wait()
            part[kept + 2 * bit * u] += landed[at + u].astype(F32)
        at += count
        bit *= 2
    gw_ref[...] = part[me]

    for r in range(rounds):
        blocks = pl.ds(0, heads - 1)
        sent = out_t.at[r, pl.ds(0, 3), blocks]
        pltpu.make_async_copy(sent, sent, qkv_send.at[r]).wait()
        sent = out_t.at[r, pl.ds(3, 1), blocks]
        pltpu.make_async_copy(sent, sent, g_send.at[r]).wait()
        sent = ret.at[r, :, blocks]
        pltpu.make_async_copy(sent, sent, res_send.at[r]).wait()


def flip_bits_plain(heads):
    return range(1, heads)


def bits_of(tok):
    bit = 1
    while bit < tok:
        yield bit
        bit *= 2


def local(queries, key_rows, value_rows, projected_output_gradient, out_weight, offsets):
    rounds, rows, width = queries.shape
    heads = offsets.shape[0]
    head_dim = width // heads
    tok = lax.axis_size("tok")
    phases = projected_output_gradient.shape[1] // rows
    seg = heads * rows
    own = width // tok
    dims = (rounds, rows, width, heads, head_dim, tok, phases)
    mask = (jnp.arange(phases)[:, None] == jnp.repeat(offsets, head_dim)[None, :]).astype(F32)
    vmem = pl.BlockSpec(memory_space=pltpu.VMEM)
    rows_shape = jax.ShapeDtypeStruct((rounds, rows, width), BF16)
    return pl.pallas_call(
        functools.partial(main_kernel, dims),
        out_shape=(rows_shape, rows_shape, rows_shape, jax.ShapeDtypeStruct((own, width), F32)),
        in_specs=[vmem] * 5 + [pl.BlockSpec(memory_space=pl.ANY)],
        out_specs=(vmem,) * 4,
        scratch_shapes=[
            pltpu.VMEM((rounds, rows * phases, width), BF16),
            pltpu.VMEM((rounds, 4, heads, head_dim, rows), BF16),
            pltpu.VMEM((rounds, 4, head_dim, seg), BF16),
            pltpu.VMEM((rounds, 4, head_dim, seg), BF16),
            pltpu.VMEM((rounds, 4, heads, head_dim, rows), BF16),
            pltpu.VMEM((rows, width), BF16),
            pltpu.VMEM((rows * phases, width), BF16),
            pltpu.VMEM((seg, head_dim), BF16),
            pltpu.VMEM((seg, head_dim), BF16),
            pltpu.VMEM((head_dim, seg), F32),
            pltpu.VMEM((head_dim, seg), F32),
            pltpu.VMEM((width, width), F32),
            pltpu.VMEM((tok, own, width), BF16),
            pltpu.VMEM((tok, own, width), F32),
            pltpu.VMEM((tok, own, width), BF16),
            pltpu.SemaphoreType.DMA((rounds,)),
            pltpu.SemaphoreType.DMA((rounds,)),
            pltpu.SemaphoreType.DMA((rounds,)),
            pltpu.SemaphoreType.DMA((rounds,)),
            pltpu.SemaphoreType.DMA((rounds,)),
            pltpu.SemaphoreType.DMA((rounds,)),
            pltpu.SemaphoreType.DMA((rounds,)),
            pltpu.SemaphoreType.DMA((tok,)),
            pltpu.SemaphoreType.DMA((tok,)),
        ],
        compiler_params=pltpu.CompilerParams(
            collective_id=0, has_side_effects=True, vmem_limit_bytes=64000000
        ),
        name="branch_backward",
    )(queries, key_rows, value_rows, out_weight, mask, projected_output_gradient)


def solution(mesh):
    placed = (
        P("slides", "tok", None),
        P("slides", "tok", None),
        P("slides", "tok", None),
        P("slides", "tok", None),
        P(),
        P(),
    )
    return jax.shard_map(
        local,
        mesh=mesh,
        in_specs=placed,
        out_specs=(
            P("slides", "tok", None),
            P("slides", "tok", None),
            P("slides", "tok", None),
            P(("slides", "tok"), None),
        ),
        check_vma=False,
    )
```

```python
import functools

import jax
import jax.numpy as jnp
from jax import lax
from jax.experimental import pallas as pl
from jax.experimental.pallas import tpu as pltpu
from jax.sharding import PartitionSpec as P

MESH = pl.DeviceIdType.MESH
F32 = jnp.float32
BF16 = jnp.bfloat16
LOG2E = 1.4426950408889634


def dot(a, b, ca, cb):
    return lax.dot_general(a, b, (((ca,), (cb,)), ((), ())), preferred_element_type=F32)


def flip_bits(index, mask):
    out = index
    bit = 1
    while bit <= mask:
        if mask & bit:
            out = out + bit - 2 * bit * ((index // bit) % 2)
        bit *= 2
    return out


def main_kernel(
    dims,
    q_ref, k_ref, v_ref, w_ref, mask_ref, x_hbm,
    dq_ref, dk_ref, dv_ref, gw_ref,
    x, out_t, recv, res, ret, g_rows, spread, k_rows, v_rows, dk_acc, dv_acc, term, half, part, landed,
    x_sem, qkv_send, qkv_recv, g_send, g_recv, res_send, ret_recv, attn_send, attn_recv, red_send, red_recv,
):
    rounds, rows, width, heads, head_dim, tok, phases = dims
    seg = heads * rows
    me = lax.axis_index("tok")
    lane = me % heads
    base = me - lane
    order = sorted(range(1, heads), key=lambda s: (-(s // (heads // 2)), -s))
    scale = head_dim ** (-0.5)

    for r in range(rounds):
        pltpu.make_async_copy(x_hbm.at[r], x.at[r], x_sem.at[r]).start()

    greet = sorted(set(flip_bits_plain(heads)) | set(b for b in bits_of(tok)))
    barrier = pltpu.get_barrier_semaphore()
    for s in greet:
        peer = flip_bits(me, s)
        pl.semaphore_signal(barrier, inc=1, device_id={"tok": peer}, device_id_type=MESH)
    pl.semaphore_wait(barrier, len(greet))

    def columns(d):
        return pl.ds(pl.multiple_of(d * rows, rows), rows)

    def send_out(r, first, count, send_sem, recv_sem):
        for s in order:
            d = flip_bits(lane, s)
            pltpu.make_async_remote_copy(
                src_ref=out_t.at[r, pl.ds(first, count), d],
                dst_ref=recv.at[r, pl.ds(first, count), :, columns(lane)],
                send_sem=send_sem.at[r],
                recv_sem=recv_sem.at[r],
                device_id={"tok": base + d},
                device_id_type=MESH,
            ).start()
        pltpu.make_async_copy(
            out_t.at[r, pl.ds(first, count), lane],
            recv.at[r, pl.ds(first, count), :, columns(lane)],
            recv_sem.at[r],
        ).start()

    def prepare(r, carry):
        for a, ref in enumerate((q_ref, k_ref, v_ref)):
            out_t[r, a] = ref[r].T.reshape(heads, head_dim, rows)
        send_out(r, 0, 3, qkv_send, qkv_recv)
        pltpu.make_async_copy(x_hbm.at[r], x.at[r], x_sem.at[r]).wait()

        def chunk(c, inner):
            t = pl.multiple_of(c * 256, 256)
            y = dot(x[r, pl.ds(t, 256), :], w_ref[...], 1, 0)
            y = y.reshape(256 // phases, phases, width) * mask_ref[...][None]
            i = pl.multiple_of(c * (256 // phases), 256 // phases)
            g_rows[pl.ds(i, 256 // phases), :] = jnp.sum(y, axis=1).astype(BF16)
            return inner

        lax.fori_loop(0, rows * phases // 256, chunk, 0)
        out_t[r, 3] = g_rows[...].T.reshape(heads, head_dim, rows)
        send_out(r, 3, 1, g_send, g_recv)
        return carry

    lax.fori_loop(0, rounds, prepare, 0)

    def send_back(r, first, count, send_sem, recv_sem):
        for s in order:
            d = flip_bits(lane, s)
            pltpu.make_async_remote_copy(
                src_ref=res.at[r, pl.ds(first, count), :, columns(d)],
                dst_ref=ret.at[r, pl.ds(first, count), lane],
                send_sem=send_sem.at[r],
                recv_sem=recv_sem.at[r],
                device_id={"tok": base + d},
                device_id_type=MESH,
            ).start()
        pltpu.make_async_copy(
            res.at[r, pl.ds(first, count), :, columns(lane)],
            ret.at[r, pl.ds(first, count), lane],
            recv_sem.at[r],
        ).start()

    block = 256

    def attend(r, carry):
        pltpu.make_async_copy(
            recv.at[r, pl.ds(0, 3)], recv.at[r, pl.ds(0, 3)], qkv_recv.at[r]
        ).wait()
        k_rows[...] = recv[r, 1].T
        v_rows[...] = recv[r, 2].T
        dk_acc[...] = jnp.zeros_like(dk_acc)
        dv_acc[...] = jnp.zeros_like(dv_acc)
        pltpu.make_async_copy(recv.at[r, 3], recv.at[r, 3], g_recv.at[r]).wait()

        def q_block(b, inner):
            cols = pl.ds(pl.multiple_of(b * block, block), block)
            qt = recv[r, 0, :, cols]
            gt = recv[r, 3, :, cols]
            s = dot(k_rows[...], qt, 1, 0)
            top = jnp.max(s, axis=0, keepdims=True)
            e = jnp.exp2((s - top) * (scale * LOG2E))
            inv = 1.0 / jnp.sum(e, axis=0, keepdims=True)
            p = e * inv
            p_low = p.astype(BF16)
            ot = dot(recv[r, 2], p_low, 1, 0).astype(BF16)
            res[r, 3, :, cols] = ot
            dp = dot(v_rows[...], gt, 1, 0)
            delta = jnp.sum(gt.astype(F32) * ot.astype(F32), axis=0, keepdims=True)
            ds = (p * (dp - delta)).astype(BF16)
            res[r, 0, :, cols] = (dot(recv[r, 1], ds, 1, 0) * scale).astype(BF16)
            dk_acc[...] += dot(qt, ds, 1, 1)
            dv_acc[...] += dot(gt, p_low, 1, 1)
            return inner

        lax.fori_loop(0, seg // block, q_block, 0)
        res[r, 1] = (dk_acc[...] * scale).astype(BF16)
        res[r, 2] = dv_acc[...].astype(BF16)
        send_back(r, 3, 1, attn_send, attn_recv)
        send_back(r, 0, 3, res_send, ret_recv)
        return carry

    lax.fori_loop(0, rounds, attend, 0)

    term[...] = jnp.zeros_like(term)
    jb = 256

    def finish(r, carry):
        pltpu.make_async_copy(ret.at[r, 3], ret.at[r, 3], attn_recv.at[r]).wait()
        g_rows[...] = ret[r, 3].reshape(width, rows).T

        def chunk(c, inner):
            n = 256 // phases
            a = g_rows[pl.ds(pl.multiple_of(c * n, n), n), :].astype(F32)
            full = a[:, None, :] * mask_ref[...][None]
            spread[pl.ds(pl.multiple_of(c * 256, 256), 256), :] = full.reshape(256, width).astype(BF16)
            return inner

        lax.fori_loop(0, rows * phases // 256, chunk, 0)

        for j in range(width // jb):
            here = pl.ds(j * jb, jb)
            term[here, :] += dot(x[r, :, here], spread[...], 0, 0)
        return carry

    lax.fori_loop(0, rounds, finish, 0)

    def lay_out(r, carry):
        got = ret.at[r, pl.ds(0, 3)]
        pltpu.make_async_copy(got, got, ret_recv.at[r]).wait()
        for a, ref in enumerate((dq_ref, dk_ref, dv_ref)):
            ref[r] = ret[r, a].reshape(width, rows).T
        return carry

    lax.fori_loop(0, rounds - 1, lay_out, 0)

    own = width // tok
    part[...] = term[...].reshape(tok, own, width)
    count = tok
    stage = 0
    bit = 1
    at = 0
    kept = 0
    while bit < tok:
        b = (me // bit) % 2
        peer = me + bit - 2 * bit * b
        count //= 2
        for u in range(count):
            half[at + u] = part[kept + bit * (1 - b) + 2 * bit * u].astype(BF16)
        for u in range(count):
            pltpu.make_async_remote_copy(
                src_ref=half.at[at + u],
                dst_ref=landed.at[at + u],
                send_sem=red_send.at[at + u],
                recv_sem=red_recv.at[at + u],
                device_id={"tok": peer},
                device_id_type=MESH,
            ).start()
        kept = kept + bit * b
        if bit == 1:
            lay_out(rounds - 1, 0)
        for u in range(count):
            pltpu.make_async_remote_copy(
                src_ref=half.at[at + u],
                dst_ref=landed.at[at + u],
                send_sem=red_send.at[at + u],
                recv_sem=red_recv.at[at + u],
                device_id={"tok": peer},
                device_id_type=MESH,
            ).wait()
            part[kept + 2 * bit * u] += landed[at + u].astype(F32)
        at += count
        bit *= 2
    gw_ref[...] = part[me]

    for r in range(rounds):
        blocks = pl.ds(0, heads - 1)
        sent = out_t.at[r, pl.ds(0, 3), blocks]
        pltpu.make_async_copy(sent, sent, qkv_send.at[r]).wait()
        sent = out_t.at[r, pl.ds(3, 1), blocks]
        pltpu.make_async_copy(sent, sent, g_send.at[r]).wait()
        sent = ret.at[r, pl.ds(0, 3), blocks]
        pltpu.make_async_copy(sent, sent, res_send.at[r]).wait()
        sent = ret.at[r, pl.ds(3, 1), blocks]
        pltpu.make_async_copy(sent, sent, attn_send.at[r]).wait()


def flip_bits_plain(heads):
    return range(1, heads)


def bits_of(tok):
    bit = 1
    while bit < tok:
        yield bit
        bit *= 2


def local(queries, key_rows, value_rows, projected_output_gradient, out_weight, offsets):
    rounds, rows, width = queries.shape
    heads = offsets.shape[0]
    head_dim = width // heads
    tok = lax.axis_size("tok")
    phases = projected_output_gradient.shape[1] // rows
    seg = heads * rows
    own = width // tok
    dims = (rounds, rows, width, heads, head_dim, tok, phases)
    mask = (jnp.arange(phases)[:, None] == jnp.repeat(offsets, head_dim)[None, :]).astype(F32)
    vmem = pl.BlockSpec(memory_space=pltpu.VMEM)
    rows_shape = jax.ShapeDtypeStruct((rounds, rows, width), BF16)
    return pl.pallas_call(
        functools.partial(main_kernel, dims),
        out_shape=(rows_shape, rows_shape, rows_shape, jax.ShapeDtypeStruct((own, width), F32)),
        in_specs=[vmem] * 5 + [pl.BlockSpec(memory_space=pl.ANY)],
        out_specs=(vmem,) * 4,
        scratch_shapes=[
            pltpu.VMEM((rounds, rows * phases, width), BF16),
            pltpu.VMEM((rounds, 4, heads, head_dim, rows), BF16),
            pltpu.VMEM((rounds, 4, head_dim, seg), BF16),
            pltpu.VMEM((rounds, 4, head_dim, seg), BF16),
            pltpu.VMEM((rounds, 4, heads, head_dim, rows), BF16),
            pltpu.VMEM((rows, width), BF16),
            pltpu.VMEM((rows * phases, width), BF16),
            pltpu.VMEM((seg, head_dim), BF16),
            pltpu.VMEM((seg, head_dim), BF16),
            pltpu.VMEM((head_dim, seg), F32),
            pltpu.VMEM((head_dim, seg), F32),
            pltpu.VMEM((width, width), F32),
            pltpu.VMEM((tok, own, width), BF16),
            pltpu.VMEM((tok, own, width), F32),
            pltpu.VMEM((tok, own, width), BF16),
            pltpu.SemaphoreType.DMA((rounds,)),
            pltpu.SemaphoreType.DMA((rounds,)),
            pltpu.SemaphoreType.DMA((rounds,)),
            pltpu.SemaphoreType.DMA((rounds,)),
            pltpu.SemaphoreType.DMA((rounds,)),
            pltpu.SemaphoreType.DMA((rounds,)),
            pltpu.SemaphoreType.DMA((rounds,)),
            pltpu.SemaphoreType.DMA((rounds,)),
            pltpu.SemaphoreType.DMA((rounds,)),
            pltpu.SemaphoreType.DMA((tok,)),
            pltpu.SemaphoreType.DMA((tok,)),
        ],
        compiler_params=pltpu.CompilerParams(
            collective_id=0, has_side_effects=True, vmem_limit_bytes=64000000
        ),
        name="branch_backward",
    )(queries, key_rows, value_rows, out_weight, mask, projected_output_gradient)


def solution(mesh):
    placed = (
        P("slides", "tok", None),
        P("slides", "tok", None),
        P("slides", "tok", None),
        P("slides", "tok", None),
        P(),
        P(),
    )
    return jax.shard_map(
        local,
        mesh=mesh,
        in_specs=placed,
        out_specs=(
            P("slides", "tok", None),
            P("slides", "tok", None),
            P("slides", "tok", None),
            P(("slides", "tok"), None),
        ),
        check_vma=False,
    )
```
